32 devices in a mesh: ctx: 8 (over y, x, core), fsdp: 4 (over z).
Axes of the slice: x: 2, y: 2, z: 4, core: 2. Of those that a mesh axis runs over, the one named last changes fastest.
Arguments:
- inputs: bfloat16 [4, 2048, 1536], P('fsdp', 'ctx'), may hold values from -6 to 6
- cotangent: bfloat16 [4, 2048, 1536], P('fsdp', 'ctx'), may hold values from -6 to 6
- positions: int32 [2048], replicated, may hold values from 0 to 2047, as said below
- w_query: bfloat16 [1536, 1536], P(('ctx', 'fsdp')), may hold values from -0.15625 to 0.15625
- key_weight: bfloat16 [1536, 256], P(('ctx', 'fsdp')), may hold values from -0.15625 to 0.15625
- value_weight: bfloat16 [1536, 256], P(('ctx', 'fsdp')), may hold values from -0.15625 to 0.15625
- w_out: bfloat16 [1536, 1536], P(('ctx', 'fsdp')), may hold values from -0.5 to 0.5
- b_query: bfloat16 [1536], P(('ctx', 'fsdp')), may hold values from -3 to 3
- key_bias_vector: bfloat16 [256], P(('ctx', 'fsdp')), may hold values from -3 to 3
- value_bias_vector: bfloat16 [256], P(('ctx', 'fsdp')), may hold values from -3 to 3
- gain_attn: bfloat16 [1536], P(('ctx', 'fsdp')), may hold values from 0.5 to 1.5
- gain_ffn: bfloat16 [1536], P(('ctx', 'fsdp')), may hold values from 0.5 to 1.5
- w_gate: bfloat16 [1536, 8960], P(None, ('ctx', 'fsdp')), may hold values from -0.15625 to 0.15625
- w_up: bfloat16 [1536, 8960], P(None, ('ctx', 'fsdp')), may hold values from -0.15625 to 0.15625
- w_down: bfloat16 [1536, 8960], P(None, ('ctx', 'fsdp')), may hold values from -0.0625 to 0.0625
Outputs:
- outputs: bfloat16 [4, 2048, 1536], P('fsdp', 'ctx')
- input_grad: float32 [4, 2048, 1536], P('fsdp', 'ctx')
- w_query_grad: float32 [1536, 1536], P(('ctx', 'fsdp'))
- w_key_grad: float32 [1536, 256], P(('ctx', 'fsdp'))
- w_value_grad: float32 [1536, 256], P(('ctx', 'fsdp'))
- w_out_grad: float32 [1536, 1536], P(('ctx', 'fsdp'))
- b_query_grad: float32 [1536], P(('ctx', 'fsdp'))
- b_key_grad: float32 [256], P(('ctx', 'fsdp'))
- b_value_grad: float32 [256], P(('ctx', 'fsdp'))
- gain_attn_grad: float32 [1536], P(('ctx', 'fsdp'))
- gain_ffn_grad: float32 [1536], P(('ctx', 'fsdp'))
- w_gate_grad: float32 [1536, 8960], P(None, ('ctx', 'fsdp'))
- w_up_grad: float32 [1536, 8960], P(None, ('ctx', 'fsdp'))
- w_down_grad: float32 [1536, 8960], P(None, ('ctx', 'fsdp'))
The draws below stay inside these ranges and needn't reach their ends.
Inputs may be any that keep to these rules, and one draw needn't show every extreme that they name: positions holds every position of a sequence once; the stored rows come in aligned pairs of blocks of 128 rows with consecutive positions, an early block number b first and then the block numbered 2048 / 128 - 1 - b; the early block of each pair differs from pair to pair.
All inputs are finite; a program needn't handle non-finite values.
Results may differ from the reference program's by a relative error of at most 0.028.
Values may be sent and summed in bfloat16 or wider, within the bound.
No kernel may reach another device: no remote copies, remote signals or barrier semaphores. Data moves between devices by JAX's collectives and lax.ppermute only.
A program may use at most 320 MiB of HBM per device.

```python
import jax
import jax.numpy as jnp
from jax import lax

MODEL_WIDTH = 1536
QUERY_HEADS = 12
KEY_VALUE_HEADS = 2
HEAD_SIZE = 128
HIDDEN_UNITS = 8960
BLK = 128
SEQ = 2048
SEQS = 4


def draw_positions(key, part):
    blocks_half = SEQ // (2 * BLK)
    ranking = jax.random.permutation(key, blocks_half).astype(jnp.int32)
    late_blocks = 2 * blocks_half - 1 - ranking
    block_ids = jnp.stack([ranking, late_blocks], axis=1).reshape(-1)
    offsets = jnp.arange(BLK, dtype=jnp.int32)
    return (block_ids[:, None] * BLK + offsets[None, :]).reshape(-1).astype(jnp.int32)


def block_scale(rng, extent, shards, smallest, top_value):
    factor_of, own = 1.0, jax.random.fold_in(rng, 6)
    for axis_at, parts in shards:
        heights = jnp.exp(jax.random.uniform(jax.random.fold_in(own, axis_at), (parts,), jnp.float32, smallest / len(shards), top_value / len(shards)))
        factor_of = factor_of * jnp.repeat(heights, extent[axis_at] // parts).reshape([-1 if axis == axis_at else 1 for axis in range(len(extent))])
    return factor_of


def normal_values(rng, dims, spread, reach, pieces=(), held_as=jnp.bfloat16):
    loudness = block_scale(rng, dims, pieces, -0.22, 0.18) if pieces else 1.0
    drawn = jax.random.normal(rng, dims, jnp.float32) * spread * loudness
    return jnp.minimum(jnp.maximum(drawn, -reach), reach).astype(held_as)


def setup_inputs(seed: int = 0) -> dict:
    keys = jax.random.split(jax.random.key(seed), 16)
    return {
        "inputs": normal_values(keys[0], (SEQS, SEQ, MODEL_WIDTH), 1.0, 6.0, ((0, 4), (1, 8))),
        "cotangent": normal_values(keys[1], (SEQS, SEQ, MODEL_WIDTH), 1.0, 6.0, ((0, 4), (1, 8))),
        "positions": draw_positions(jax.random.fold_in(keys[15], 71), 0),
        "w_query": normal_values(keys[3], (MODEL_WIDTH, QUERY_HEADS * HEAD_SIZE), MODEL_WIDTH ** -0.5, 0.15625, ((0, 32),)),
        "key_weight": normal_values(keys[4], (MODEL_WIDTH, KEY_VALUE_HEADS * HEAD_SIZE), MODEL_WIDTH ** -0.5, 0.15625, ((0, 32),)),
        "value_weight": normal_values(keys[5], (MODEL_WIDTH, KEY_VALUE_HEADS * HEAD_SIZE), MODEL_WIDTH ** -0.5, 0.15625, ((0, 32),)),
        "w_out": normal_values(keys[6], (MODEL_WIDTH, QUERY_HEADS * HEAD_SIZE), HEAD_SIZE ** -0.5, 0.5, ((0, 32),)),
        "b_query": normal_values(keys[7], (QUERY_HEADS * HEAD_SIZE,), 0.5, 3.0, ((0, 32),)),
        "key_bias_vector": normal_values(keys[8], (KEY_VALUE_HEADS * HEAD_SIZE,), 0.5, 3.0, ((0, 32),)),
        "value_bias_vector": normal_values(keys[9], (KEY_VALUE_HEADS * HEAD_SIZE,), 0.5, 3.0, ((0, 32),)),
        "gain_attn": jnp.clip(1.0 + 0.1 * jax.random.normal(keys[10], (MODEL_WIDTH,), jnp.float32), 0.5, 1.5).astype(jnp.bfloat16),
        "gain_ffn": jnp.clip(1.0 + 0.1 * jax.random.normal(keys[11], (MODEL_WIDTH,), jnp.float32), 0.5, 1.5).astype(jnp.bfloat16),
        "w_gate": normal_values(keys[12], (MODEL_WIDTH, HIDDEN_UNITS), MODEL_WIDTH ** -0.5, 0.15625, ((1, 32),)),
        "w_up": normal_values(keys[13], (MODEL_WIDTH, HIDDEN_UNITS), MODEL_WIDTH ** -0.5, 0.15625, ((1, 32),)),
        "w_down": normal_values(keys[14], (MODEL_WIDTH, HIDDEN_UNITS), HIDDEN_UNITS ** -0.5, 0.0625, ((1, 32),)),
    }


NORM_EPS = 1e-06
ROPE_BASE = 1000000.0

def rope_tables(places, width):
    half_width = width // 2
    frequency = ROPE_BASE ** (-(jnp.arange(half_width, dtype=jnp.float32) * 2.0 / width))
    angles = places.astype(jnp.float32)[:, None] * frequency[None, :]
    cosine_table = jnp.concatenate([jnp.cos(angles), jnp.cos(angles)], -1)
    sine_values = jnp.concatenate([jnp.sin(angles), jnp.sin(angles)], -1)
    return (cosine_table[:, None, :], sine_values[:, None, :])

def apply_rotary(source, cosine_table, sine_values):
    half_width = source.shape[-1] // 2
    turned = jnp.concatenate([-source[..., half_width:], source[..., :half_width]], -1)
    return source * cosine_table + turned * sine_values

def undo_rotary(source, cosine_table, sine_values):
    weighted = source * sine_values
    half_width = source.shape[-1] // 2
    returned = jnp.concatenate([weighted[..., half_width:], -weighted[..., :half_width]], -1)
    return source * cosine_table + returned

def norm_back(upstream, source, inverse, gain_vec):
    scaled = upstream * gain_vec
    return inverse * scaled - source * inverse ** 3 * lax.optimization_barrier(jnp.mean(scaled * source, -1, keepdims=True))

def reference(inputs, cotangent, positions, w_query, key_weight, value_weight, w_out, b_query, key_bias_vector, value_bias_vector, gain_attn, gain_ffn, w_gate, w_up, w_down):
    queries_per_group = QUERY_HEADS // KEY_VALUE_HEADS
    score_scale = HEAD_SIZE ** (-0.5)
    cosine_table, sine_values = rope_tables(positions, HEAD_SIZE)
    visible = positions[None, :] <= positions[:, None]
    attn_gain = gain_attn.astype(jnp.float32)
    ffn_gain = gain_ffn.astype(jnp.float32)
    query_bias = b_query.astype(jnp.float32)
    key_bias = key_bias_vector.astype(jnp.float32)
    value_bias = value_bias_vector.astype(jnp.float32)

    def head_forward(packed):
        query_one, key_one, value_one = packed
        scores = jnp.dot(query_one, key_one.T, preferred_element_type=jnp.float32) * score_scale
        scores = jnp.where(visible, scores, -jnp.inf)
        row_max = lax.optimization_barrier(jnp.max(scores, -1, keepdims=True))
        log_total = row_max + jnp.log(lax.optimization_barrier(jnp.sum(jnp.exp(scores - row_max), -1, keepdims=True)))
        probs = jnp.exp(scores - log_total).astype(jnp.bfloat16)
        return (jnp.dot(probs, value_one, preferred_element_type=jnp.float32).astype(jnp.bfloat16), log_total)

    def head_backward(packed):
        query_one, key_one, value_one, out_one, d_out_one, log_total = packed
        scores = jnp.dot(query_one, key_one.T, preferred_element_type=jnp.float32) * score_scale
        scores = jnp.where(visible, scores, -jnp.inf)
        probs_exact = jnp.exp(scores - log_total)
        probs_bf = probs_exact.astype(jnp.bfloat16)
        value_gradient = jnp.dot(probs_bf.T, d_out_one, preferred_element_type=jnp.float32)
        d_probs = jnp.dot(d_out_one, value_one.T, preferred_element_type=jnp.float32)
        delta = lax.optimization_barrier(jnp.sum(d_out_one.astype(jnp.float32) * out_one.astype(jnp.float32), -1, keepdims=True))
        d_scores = (probs_exact * (d_probs - delta) * score_scale).astype(jnp.bfloat16)
        d_query = jnp.dot(d_scores, key_one, preferred_element_type=jnp.float32)
        key_gradient = jnp.dot(d_scores.T, query_one, preferred_element_type=jnp.float32)
        return (d_query, key_gradient, value_gradient)

    def one_sequence(totals, sequence_pair):
        x_rows, cot_rows = sequence_pair
        hidden = x_rows.astype(jnp.float32)
        inverse_attn = lax.rsqrt(lax.optimization_barrier(jnp.mean(hidden * hidden, -1, keepdims=True)) + NORM_EPS)
        normed_attn = (hidden * inverse_attn * attn_gain).astype(jnp.bfloat16)
        queries = jnp.dot(normed_attn, w_query, preferred_element_type=jnp.float32) + query_bias
        local_keys = jnp.dot(normed_attn, key_weight, preferred_element_type=jnp.float32) + key_bias
        local_values = jnp.dot(normed_attn, value_weight, preferred_element_type=jnp.float32) + value_bias
        query_rot = apply_rotary(queries.reshape(-1, QUERY_HEADS, HEAD_SIZE), cosine_table, sine_values).astype(jnp.bfloat16)
        key_rotated = apply_rotary(local_keys.reshape(-1, KEY_VALUE_HEADS, HEAD_SIZE), cosine_table, sine_values).astype(jnp.bfloat16)
        rows_of_value = local_values.astype(jnp.bfloat16).reshape(-1, KEY_VALUE_HEADS, HEAD_SIZE)
        query_heads = query_rot.transpose(1, 0, 2)
        heads_of_key = jnp.repeat(key_rotated.transpose(1, 0, 2), queries_per_group, axis=0)
        heads_of_value = jnp.repeat(rows_of_value.transpose(1, 0, 2), queries_per_group, axis=0)
        attn_heads, log_totals = lax.map(head_forward, (query_heads, heads_of_key, heads_of_value))
        attn_out = attn_heads.transpose(1, 0, 2).reshape(-1, QUERY_HEADS * HEAD_SIZE)
        middle = hidden + jnp.dot(attn_out, w_out.T, preferred_element_type=jnp.float32)
        inverse_ffn = lax.rsqrt(lax.optimization_barrier(jnp.mean(middle * middle, -1, keepdims=True)) + NORM_EPS)
        normed_ffn = (middle * inverse_ffn * ffn_gain).astype(jnp.bfloat16)
        gate_pre = jnp.dot(normed_ffn, w_gate, preferred_element_type=jnp.float32)
        up_proj = jnp.dot(normed_ffn, w_up, preferred_element_type=jnp.float32)
        sigmoid_gate = jax.nn.sigmoid(gate_pre)
        swish = gate_pre * sigmoid_gate
        activated = (swish * up_proj).astype(jnp.bfloat16)
        outputs = (middle + jnp.dot(activated, w_down.T, preferred_element_type=jnp.float32)).astype(jnp.bfloat16)
        grad_down = jnp.dot(cot_rows.T, activated, preferred_element_type=jnp.float32)
        d_act = jnp.dot(cot_rows, w_down, preferred_element_type=jnp.float32)
        d_gate = (d_act * up_proj * sigmoid_gate * (1.0 + gate_pre * (1.0 - sigmoid_gate))).astype(jnp.bfloat16)
        d_up = (d_act * swish).astype(jnp.bfloat16)
        grad_gate = jnp.dot(normed_ffn.T, d_gate, preferred_element_type=jnp.float32)
        grad_up = jnp.dot(normed_ffn.T, d_up, preferred_element_type=jnp.float32)
        d_normed_ffn = jnp.dot(d_gate, w_gate.T, preferred_element_type=jnp.float32) + jnp.dot(d_up, w_up.T, preferred_element_type=jnp.float32)
        grad_gain_ffn = lax.optimization_barrier(jnp.sum(d_normed_ffn * middle * inverse_ffn, 0))
        d_middle = cot_rows.astype(jnp.float32) + norm_back(d_normed_ffn, middle, inverse_ffn, ffn_gain)
        d_middle_b = d_middle.astype(jnp.bfloat16)
        grad_out = jnp.dot(d_middle_b.T, attn_out, preferred_element_type=jnp.float32)
        d_attn = jnp.dot(d_middle_b, w_out, preferred_element_type=jnp.float32).astype(jnp.bfloat16)
        d_heads = d_attn.reshape(-1, QUERY_HEADS, HEAD_SIZE).transpose(1, 0, 2)
        dq_heads, key_gradient_heads, value_gradient_heads = lax.map(head_backward, (query_heads, heads_of_key, heads_of_value, attn_heads, d_heads, log_totals))
        d_query = undo_rotary(dq_heads.transpose(1, 0, 2), cosine_table, sine_values).reshape(-1, QUERY_HEADS * HEAD_SIZE)
        key_gradient_sum = key_gradient_heads.reshape(KEY_VALUE_HEADS, queries_per_group, -1, HEAD_SIZE).sum(1).transpose(1, 0, 2)
        key_gradient = undo_rotary(key_gradient_sum, cosine_table, sine_values).reshape(-1, KEY_VALUE_HEADS * HEAD_SIZE)
        value_gradient = value_gradient_heads.reshape(KEY_VALUE_HEADS, queries_per_group, -1, HEAD_SIZE).sum(1).transpose(1, 0, 2).reshape(-1, KEY_VALUE_HEADS * HEAD_SIZE)
        grad_qbias = lax.optimization_barrier(jnp.sum(d_query, 0))
        grad_kbias = lax.optimization_barrier(jnp.sum(key_gradient, 0))
        grad_vbias = lax.optimization_barrier(jnp.sum(value_gradient, 0))
        query_b = d_query.astype(jnp.bfloat16)
        key_b = key_gradient.astype(jnp.bfloat16)
        value_b = value_gradient.astype(jnp.bfloat16)
        grad_query = jnp.dot(normed_attn.T, query_b, preferred_element_type=jnp.float32)
        grad_key = jnp.dot(normed_attn.T, key_b, preferred_element_type=jnp.float32)
        grad_value = jnp.dot(normed_attn.T, value_b, preferred_element_type=jnp.float32)
        d_normed_attn = jnp.dot(query_b, w_query.T, preferred_element_type=jnp.float32) + jnp.dot(key_b, key_weight.T, preferred_element_type=jnp.float32) + jnp.dot(value_b, value_weight.T, preferred_element_type=jnp.float32)
        grad_gain_attn = lax.optimization_barrier(jnp.sum(d_normed_attn * hidden * inverse_attn, 0))
        input_grad = d_middle + norm_back(d_normed_attn, hidden, inverse_attn, attn_gain)
        terms = (grad_query, grad_key, grad_value, grad_out, grad_qbias, grad_kbias, grad_vbias, grad_gain_attn, grad_gain_ffn, grad_gate, grad_up, grad_down)
        updated = tuple((left + right for left, right in zip(totals, terms)))
        return (updated, (outputs, input_grad))
    empty_sums = (jnp.zeros((MODEL_WIDTH, QUERY_HEADS * HEAD_SIZE), jnp.float32), jnp.zeros((MODEL_WIDTH, KEY_VALUE_HEADS * HEAD_SIZE), jnp.float32), jnp.zeros((MODEL_WIDTH, KEY_VALUE_HEADS * HEAD_SIZE), jnp.float32), jnp.zeros((MODEL_WIDTH, QUERY_HEADS * HEAD_SIZE), jnp.float32), jnp.zeros((QUERY_HEADS * HEAD_SIZE,), jnp.float32), jnp.zeros((KEY_VALUE_HEADS * HEAD_SIZE,), jnp.float32), jnp.zeros((KEY_VALUE_HEADS * HEAD_SIZE,), jnp.float32), jnp.zeros((MODEL_WIDTH,), jnp.float32), jnp.zeros((MODEL_WIDTH,), jnp.float32), jnp.zeros((MODEL_WIDTH, HIDDEN_UNITS), jnp.float32), jnp.zeros((MODEL_WIDTH, HIDDEN_UNITS), jnp.float32), jnp.zeros((MODEL_WIDTH, HIDDEN_UNITS), jnp.float32))
    sums, (outputs, input_grad) = lax.scan(one_sequence, empty_sums, (inputs, cotangent))
    return (outputs, input_grad, sums[0], sums[1], sums[2], sums[3], sums[4], sums[5], sums[6], sums[7], sums[8], sums[9], sums[10], sums[11])
```

```python
import jax
import jax.numpy as jnp
from jax import lax
from jax.sharding import PartitionSpec as P

QUERY_HEADS = 12
KEY_VALUE_HEADS = 2
HEAD_SIZE = 128

NORM_EPS = 1e-06
ROPE_BASE = 1000000.0
BF = jnp.bfloat16
F32 = jnp.float32


def rope_tables(places, width):
    half_width = width // 2
    frequency = ROPE_BASE ** (-(jnp.arange(half_width, dtype=F32) * 2.0 / width))
    angles = places.astype(F32)[:, None] * frequency[None, :]
    cosine_table = jnp.concatenate([jnp.cos(angles), jnp.cos(angles)], -1)
    sine_values = jnp.concatenate([jnp.sin(angles), jnp.sin(angles)], -1)
    return (cosine_table[:, None, :], sine_values[:, None, :])


def apply_rotary(source, cosine_table, sine_values):
    half_width = source.shape[-1] // 2
    turned = jnp.concatenate([-source[..., half_width:], source[..., :half_width]], -1)
    return source * cosine_table + turned * sine_values


def undo_rotary(source, cosine_table, sine_values):
    weighted = source * sine_values
    half_width = source.shape[-1] // 2
    returned = jnp.concatenate([weighted[..., half_width:], -weighted[..., :half_width]], -1)
    return source * cosine_table + returned


def norm_back(upstream, source, inverse, gain_vec):
    scaled = upstream * gain_vec
    return inverse * scaled - source * inverse**3 * jnp.mean(scaled * source, -1, keepdims=True)


def dot_nn(a, b):
    return jnp.einsum("mk,kn->mn", a, b, preferred_element_type=F32)


def dot_nt(a, b):
    return jnp.einsum("mk,nk->mn", a, b, preferred_element_type=F32)


def dot_tn(a, b):
    return jnp.einsum("km,kn->mn", a, b, preferred_element_type=F32)


def swap(value, bit):
    n = lax.axis_size("ctx")
    return lax.ppermute(value, "ctx", [(i, i ^ bit) for i in range(n)])


def high_bits():
    n = lax.axis_size("ctx")
    bits = []
    b = 8
    while b < n:
        bits.append(b)
        b *= 2
    return bits


def unit_order():
    order = [0]
    for b in high_bits():
        order = order + [j ^ b for j in order]
    return order


def plane_order():
    return [j ^ b for b in (0, 2, 4, 6) for j in unit_order()]


def split_rows(rows):
    return (rows // 2 + 7) // 8 * 8


def gather_plane(piece):
    unit = piece
    for b in high_bits():
        unit = jnp.concatenate([unit, swap(unit, b)], 0)
    h = split_rows(unit.shape[0])
    from_x = swap(unit, 2)
    from_y = swap(unit, 4)
    top = swap(from_x[:h], 4)
    bottom = swap(from_y[h:], 2)
    return [unit, from_x, from_y, top, bottom]


def scatter_plane(mine, theirs):
    rows = mine.shape[0] // 4
    h = split_rows(rows)
    total = mine.astype(F32) + theirs.astype(F32)
    own, to_x, to_y, to_d = (total[i * rows : (i + 1) * rows] for i in range(4))
    from_x = swap(to_d[:h].astype(BF), 2)
    from_y = swap(to_d[h:].astype(BF), 4)
    to_x = jnp.concatenate([to_x[:h], to_x[h:] + from_y.astype(F32)], 0)
    to_y = jnp.concatenate([to_y[:h] + from_x.astype(F32), to_y[h:]], 0)
    got_x = swap(to_x.astype(BF), 2)
    got_y = swap(to_y.astype(BF), 4)
    total = own + got_x.astype(F32) + got_y.astype(F32)
    for b in reversed(high_bits()):
        half = total.shape[0] // 2
        total = total[:half] + swap(total[half:].astype(BF), b).astype(F32)
    return total


def place(pieces, offsets, rows):
    out = jnp.zeros((rows,) + pieces[0].shape[1:], pieces[0].dtype)
    for piece, offset in zip(pieces, offsets):
        out = lax.dynamic_update_slice_in_dim(out, piece, offset, 0)
    return out


def gather_rows(piece):
    n = lax.axis_size("ctx")
    me = lax.axis_index("ctx")
    rows = piece.shape[0]
    plane = gather_plane(piece)
    order = unit_order()
    h = split_rows(plane[0].shape[0])
    pieces, offsets = [], []
    for core in (0, 1):
        if core:
            plane = [swap(p, 1) for p in plane]
        full = plane[:3] + [jnp.concatenate(plane[3:], 0)]
        for b, unit in zip((0, 2, 4, 6), full):
            for k, j in enumerate(order):
                pieces.append(unit[k * rows : (k + 1) * rows])
                offsets.append((me ^ (j ^ b ^ core)) * rows)
    return place(pieces, offsets, n * rows)


def scatter_rows(full):
    n = lax.axis_size("ctx")
    me = lax.axis_index("ctx")
    rows = full.shape[0] // n
    take = lambda j: lax.dynamic_slice_in_dim(full, (me ^ j) * rows, rows, 0)
    order = plane_order()
    away = jnp.concatenate([take(j ^ 1) for j in order], 0).astype(BF)
    mine = jnp.concatenate([take(j) for j in order], 0)
    return scatter_plane(mine, swap(away, 1))


def scatter_fsdp(full):
    n = lax.axis_size("fsdp")
    me = lax.axis_index("fsdp")
    rows = full.shape[0] // n
    total = lax.dynamic_slice_in_dim(full, me * rows, rows, 0).astype(F32)
    for k in range(1, n):
        part = lax.dynamic_slice_in_dim(full, (me + k) % n * rows, rows, 0).astype(BF)
        total = total + lax.ppermute(part, "fsdp", [(i, (i + k) % n) for i in range(n)]).astype(F32)
    return total


def as_column(vector, rows):
    return jnp.pad(vector, (0, rows - vector.shape[0]))[:, None]


def body(
    inputs,
    cotangent,
    positions,
    w_query,
    key_weight,
    value_weight,
    w_out,
    b_query,
    key_bias_vector,
    value_bias_vector,
    gain_attn,
    gain_ffn,
    w_gate,
    w_up,
    w_down,
):
    nc = lax.axis_size("ctx")
    me = lax.axis_index("ctx")
    token_rows = inputs.shape[1]
    width = inputs.shape[2]
    qw = w_query.shape[1]
    kw = key_weight.shape[1]
    shard = w_query.shape[0]
    kshard = key_bias_vector.shape[0]
    queries_per_group = QUERY_HEADS // KEY_VALUE_HEADS
    score_scale = HEAD_SIZE ** (-0.5)
    hidden = inputs[0].astype(F32)
    cot_rows = cotangent[0]

    small = jnp.stack(
        [
            b_query,
            gain_attn,
            gain_ffn,
            jnp.pad(key_bias_vector, (0, shard - kshard)),
            jnp.pad(value_bias_vector, (0, shard - kshard)),
        ],
        1,
    )
    small = jnp.pad(small, ((0, 0), (0, 128 - small.shape[1])))
    packed = jnp.concatenate([w_query, key_weight, value_weight, small, w_out], 1)
    packed = lax.all_gather(packed, "fsdp", axis=0, tiled=True)
    cot_all = lax.all_gather(cot_rows, "fsdp", axis=0, tiled=True)
    first_cols = qw + 2 * kw + 128
    qkv_full = gather_rows(packed[:, :first_cols])
    out_full = gather_rows(packed[:, first_cols:])
    smalls = qkv_full[:, qw + 2 * kw :].T.astype(F32)
    bias_q = smalls[0:1]
    attn_gain_vec = smalls[1:2]
    ffn_gain_vec = smalls[2:3]
    unpad = lambda row: row.reshape(-1, shard)[:, :kshard].reshape(1, -1)
    bias_k = unpad(smalls[3])
    bias_v = unpad(smalls[4])

    row_offset = me * token_rows
    own_places = lax.dynamic_slice_in_dim(positions, row_offset, token_rows)
    cosine_table, sine_values = rope_tables(own_places, HEAD_SIZE)
    key_order = plane_order() + [j ^ 1 for j in plane_order()]
    key_places = jnp.concatenate(
        [lax.dynamic_slice_in_dim(positions, (me ^ j) * token_rows, token_rows) for j in key_order]
    )
    visible = own_places[:, None] >= key_places[None, :]

    inverse_attn = lax.rsqrt(jnp.mean(hidden * hidden, -1, keepdims=True) + NORM_EPS)
    normed_attn = (hidden * inverse_attn * attn_gain_vec).astype(BF)
    qkv = dot_nn(normed_attn, qkv_full[:, : qw + 2 * kw])
    queries = qkv[:, :qw] + bias_q
    local_keys = qkv[:, qw : qw + kw] + bias_k
    local_values = qkv[:, qw + kw :] + bias_v
    query_rot = apply_rotary(
        queries.reshape(token_rows, QUERY_HEADS, HEAD_SIZE), cosine_table, sine_values
    ).astype(BF)
    key_rotated = (
        apply_rotary(
            local_keys.reshape(token_rows, KEY_VALUE_HEADS, HEAD_SIZE), cosine_table, sine_values
        )
        .astype(BF)
        .reshape(token_rows, kw)
    )
    kv = jnp.concatenate([key_rotated, local_values.astype(BF)], 1)
    kv_half = jnp.concatenate(gather_plane(kv), 0)
    kv_all = jnp.concatenate([kv_half, swap(kv_half, 1)], 0)
    sequence_rows = kv_all.shape[0]
    heads_of_key = kv_all[:, :kw].reshape(sequence_rows, KEY_VALUE_HEADS, HEAD_SIZE)
    heads_of_value = kv_all[:, kw:].reshape(sequence_rows, KEY_VALUE_HEADS, HEAD_SIZE)

    def gather_hidden(weight):
        half = jnp.concatenate(gather_plane(weight.T), 0)
        return [half, swap(half, 1)]

    down = gather_hidden(w_down)
    gate = gather_hidden(w_gate)
    up = gather_hidden(w_up)

    attn_parts = []
    log_totals = []
    for key_value_head in range(KEY_VALUE_HEADS):
        query_group = query_rot[
            :, key_value_head * queries_per_group : (key_value_head + 1) * queries_per_group
        ]
        scores = (
            jnp.einsum(
                "tjd,sd->jts",
                query_group,
                heads_of_key[:, key_value_head],
                preferred_element_type=F32,
            )
            * score_scale
        )
        scores = jnp.where(visible[None], scores, -jnp.inf)
        row_max = jnp.max(scores, -1, keepdims=True)
        log_total = row_max + jnp.log(jnp.sum(jnp.exp(scores - row_max), -1, keepdims=True))
        probs = jnp.exp(scores - log_total).astype(BF)
        attn_parts.append(
            jnp.einsum(
                "jts,sd->tjd", probs, heads_of_value[:, key_value_head], preferred_element_type=F32
            ).astype(BF)
        )
        log_totals.append(log_total)
    attn_heads = jnp.concatenate(attn_parts, axis=1)
    attn_out = attn_heads.reshape(token_rows, qw)
    middle = hidden + dot_nt(attn_out, out_full)
    inverse_ffn = lax.rsqrt(jnp.mean(middle * middle, -1, keepdims=True) + NORM_EPS)
    normed_ffn = (middle * inverse_ffn * ffn_gain_vec).astype(BF)

    rows_all = lax.all_gather(normed_ffn, "fsdp", axis=0, tiled=True)
    ffn_part = None
    d_normed_part = None
    act, d_gate, d_up = [], [], []
    for half in (0, 1):
        gate_pre = dot_nt(rows_all, gate[half])
        up_proj = dot_nt(rows_all, up[half])
        d_act = dot_nt(cot_all, down[half])
        sigmoid_gate = jax.nn.sigmoid(gate_pre)
        swish = gate_pre * sigmoid_gate
        act.append((swish * up_proj).astype(BF))
        d_gate.append(
            (d_act * up_proj * sigmoid_gate * (1.0 + gate_pre * (1.0 - sigmoid_gate))).astype(BF)
        )
        d_up.append((d_act * swish).astype(BF))
    d_normed_part = (
        dot_nn(d_gate[0], gate[0])
        + dot_nn(d_up[0], up[0])
        + dot_nn(d_gate[1], gate[1])
        + dot_nn(d_up[1], up[1])
    )
    d_normed_ffn = lax.psum_scatter(
        d_normed_part.astype(BF), "fsdp", scatter_dimension=0, tiled=True
    ).astype(F32)
    ffn_part = dot_nn(act[0], down[0]) + dot_nn(act[1], down[1])
    ffn_out = lax.psum_scatter(
        ffn_part.astype(BF), "fsdp", scatter_dimension=0, tiled=True
    ).astype(F32)
    outputs = (middle + ffn_out).astype(BF)

    def hidden_grad(coefficients, rows):
        away = swap(dot_tn(coefficients[1], rows).astype(BF), 1)
        mine = dot_tn(coefficients[0], rows).astype(BF)
        return scatter_plane(mine, away).T

    grad_down = hidden_grad(act, cot_all)
    grad_gate = hidden_grad(d_gate, rows_all)
    grad_up = hidden_grad(d_up, rows_all)

    grad_gain_ffn = jnp.sum(d_normed_ffn * middle * inverse_ffn, 0)
    d_middle = cot_rows.astype(F32) + norm_back(d_normed_ffn, middle, inverse_ffn, ffn_gain_vec)
    d_middle_b = d_middle.astype(BF)
    grad_out = dot_tn(d_middle_b, attn_out)
    grad_out = scatter_fsdp(scatter_rows(grad_out))
    d_attn = dot_nn(d_middle_b, out_full).astype(BF).reshape(token_rows, QUERY_HEADS, HEAD_SIZE)
    dq_parts = []
    key_gradient_pieces = []
    value_gradient_pieces = []
    for key_value_head in range(KEY_VALUE_HEADS):
        head_slice = slice(
            key_value_head * queries_per_group, (key_value_head + 1) * queries_per_group
        )
        query_group = query_rot[:, head_slice]
        key_one = heads_of_key[:, key_value_head]
        value_one = heads_of_value[:, key_value_head]
        scores = (
            jnp.einsum("tjd,sd->jts", query_group, key_one, preferred_element_type=F32)
            * score_scale
        )
        scores = jnp.where(visible[None], scores, -jnp.inf)
        probs_exact = jnp.exp(scores - log_totals[key_value_head])
        probs_bf = probs_exact.astype(BF)
        d_group = d_attn[:, head_slice]
        out_group = attn_heads[:, head_slice]
        value_gradient_pieces.append(
            jnp.einsum("jts,tjd->sd", probs_bf, d_group, preferred_element_type=F32)
        )
        d_probs = jnp.einsum("tjd,sd->jts", d_group, value_one, preferred_element_type=F32)
        delta = jnp.sum(d_group.astype(F32) * out_group.astype(F32), -1).T[:, :, None]
        d_scores = (probs_exact * (d_probs - delta) * score_scale).astype(BF)
        dq_parts.append(jnp.einsum("jts,sd->tjd", d_scores, key_one, preferred_element_type=F32))
        key_gradient_pieces.append(
            jnp.einsum("jts,tjd->sd", d_scores, query_group, preferred_element_type=F32)
        )
    d_query_rot = jnp.concatenate(dq_parts, axis=1)
    dkv = jnp.concatenate(key_gradient_pieces + value_gradient_pieces, 1)
    half_rows = sequence_rows // 2
    dkv_own = scatter_plane(dkv[:half_rows], swap(dkv[half_rows:].astype(BF), 1))
    d_query = undo_rotary(d_query_rot, cosine_table, sine_values).reshape(token_rows, qw)
    key_gradient = undo_rotary(
        dkv_own[:, :kw].reshape(token_rows, KEY_VALUE_HEADS, HEAD_SIZE),
        cosine_table,
        sine_values,
    ).reshape(token_rows, kw)
    dv_own = dkv_own[:, kw:]
    query_b = d_query.astype(BF)
    key_b = key_gradient.astype(BF)
    value_b = dv_own.astype(BF)
    dqkv_b = jnp.concatenate([query_b, key_b, value_b], 1)
    grad_qkv = dot_tn(normed_attn, dqkv_b)
    d_normed_attn = dot_nt(dqkv_b, qkv_full[:, : qw + 2 * kw])
    grad_gain_attn = jnp.sum(d_normed_attn * hidden * inverse_attn, 0)
    input_grad = d_middle + norm_back(d_normed_attn, hidden, inverse_attn, attn_gain_vec)
    repad = lambda vector: jnp.pad(
        vector.reshape(-1, kshard), ((0, 0), (0, shard - kshard))
    ).reshape(-1)
    small_grads = jnp.stack(
        [
            jnp.sum(d_query, 0),
            grad_gain_attn,
            grad_gain_ffn,
            repad(jnp.sum(key_gradient, 0)),
            repad(jnp.sum(dv_own, 0)),
        ],
        1,
    )
    small_grads = jnp.pad(small_grads, ((0, 0), (0, 128 - small_grads.shape[1])))
    shares = scatter_fsdp(scatter_rows(jnp.concatenate([grad_qkv, small_grads], 1)))
    cols = shares[:, qw + 2 * kw :]
    return (
        outputs[None],
        input_grad[None],
        shares[:, :qw],
        shares[:, qw : qw + kw],
        shares[:, qw + kw : qw + 2 * kw],
        grad_out,
        cols[:, 0],
        cols[:kshard, 3],
        cols[:kshard, 4],
        cols[:, 1],
        cols[:, 2],
        grad_gate,
        grad_up,
        grad_down,
    )


def solution(mesh):
    both = ("ctx", "fsdp")
    rows = P("fsdp", "ctx", None)
    matrix = P(both, None)
    vector = P(both)
    hidden = P(None, both)
    return jax.shard_map(
        body,
        mesh=mesh,
        in_specs=(rows, rows, P()) + (matrix,) * 4 + (vector,) * 5 + (hidden,) * 3,
        out_specs=(rows, rows) + (matrix,) * 4 + (vector,) * 5 + (hidden,) * 3,
        check_vma=False,
    )
```
